32 devices in a mesh: dp: 16 (over z, y, x), seq: 2 (over core).
Axes of the slice: x: 2, y: 2, z: 4, core: 2. Of those that a mesh axis runs over, the one named last changes fastest.
Arguments:
- tokens: bfloat16 [48, 512, 768], P('dp', 'seq'), may hold values from -6 to 6
- prev_logits: bfloat16 [48, 12, 512, 512], P('dp', None, 'seq'), may hold values from -6 to 6
- segment_ids: int32 [48, 512], P('dp'), may hold values from 0 to 5, never falling along the last dimension, each value on 1 to 192 neighbouring positions
- out_cotangent: bfloat16 [48, 512, 768], P('dp', 'seq'), may hold values from -6 to 6
- logit_cotangent: bfloat16 [48, 12, 512, 512], P('dp', None, 'seq'), may hold values from -0.59765625 to 0.59765625
- querymap: bfloat16 [768, 768], P(('dp', 'seq')), may hold values from -0.21875 to 0.21875
- querybias: bfloat16 [768], P(('dp', 'seq')), may hold values from -3 to 3
- keymap: bfloat16 [768, 768], P(('dp', 'seq')), may hold values from -0.21875 to 0.21875
- valuemap: bfloat16 [768, 768], P(('dp', 'seq')), may hold values from -0.21875 to 0.21875
- valuebias: bfloat16 [768], P(('dp', 'seq')), may hold values from -3 to 3
- mixmap: bfloat16 [768, 768], P(('dp', 'seq')), may hold values from -1.75 to 1.75
- mixbias: bfloat16 [768], P(('dp', 'seq')), may hold values from -3 to 3
- normgain: bfloat16 [768], P(('dp', 'seq')), may hold values from 0.5 to 1.5
- normbias: bfloat16 [768], P(('dp', 'seq')), may hold values from -3 to 3
- expandmap: bfloat16 [768, 3072], P(('dp', 'seq')), may hold values from -0.21875 to 0.21875
- expandbias: bfloat16 [3072], P(('dp', 'seq')), may hold values from -3 to 3
- shrinkmap: bfloat16 [3072, 768], P(('dp', 'seq')), may hold values from -0.109375 to 0.109375
- shrinkbias: bfloat16 [768], P(('dp', 'seq')), may hold values from -3 to 3
- outgain: bfloat16 [768], P(('dp', 'seq')), may hold values from 0.5 to 1.5
- outbias: bfloat16 [768], P(('dp', 'seq')), may hold values from -3 to 3
Outputs:
- layer_out: bfloat16 [48, 512, 768], P('dp', 'seq')
- raw_logits: bfloat16 [48, 12, 512, 512], P('dp', None, 'seq')
- tokens_grad: bfloat16 [48, 512, 768], P('dp', 'seq')
- logits_grad: bfloat16 [48, 12, 512, 512], P('dp', None, 'seq')
- querymap_grad: float32 [768, 768], P(('dp', 'seq'))
- querybias_grad: float32 [768], P(('dp', 'seq'))
- keymap_grad: float32 [768, 768], P(('dp', 'seq'))
- valuemap_grad: float32 [768, 768], P(('dp', 'seq'))
- valuebias_grad: float32 [768], P(('dp', 'seq'))
- mixmap_grad: float32 [768, 768], P(('dp', 'seq'))
- mixbias_grad: float32 [768], P(('dp', 'seq'))
- normgain_grad: float32 [768], P(('dp', 'seq'))
- normbias_grad: float32 [768], P(('dp', 'seq'))
- expandmap_grad: float32 [768, 3072], P(('dp', 'seq'))
- expandbias_grad: float32 [3072], P(('dp', 'seq'))
- shrinkmap_grad: float32 [3072, 768], P(('dp', 'seq'))
- shrinkbias_grad: float32 [768], P(('dp', 'seq'))
- outgain_grad: float32 [768], P(('dp', 'seq'))
- outbias_grad: float32 [768], P(('dp', 'seq'))
The draws below stay inside these ranges and needn't reach their ends.
Inputs may be any that keep to these rules, and one draw needn't show every extreme that they name: `segment_ids`: along each row the ids never fall; each id covers 1 to 192 slots and in each row one covers exactly that many.
All inputs are finite; a program needn't handle non-finite values.
Results may differ from the reference program's by a relative error of at most 0.014.
Values may be sent and summed in bfloat16 or wider, within the bound.
A program may use at most 192 MiB of HBM per device.

```python
import math
import jax
import jax.numpy as jnp
import numpy as np
from jax import lax

D = 768
H = 12
HD = 64
FF = 3072
SEQ_LEN = 512
ROWS = 48


def with_spikes(array, rng, source, target, blocks, factor):
    def block_of(dim):
        return (jnp.arange(array.shape[dim]) // (array.shape[dim] // blocks)).reshape((-1,) + (1,) * (array.ndim - 1 - dim))

    first = jax.random.permutation(rng, blocks)[block_of(target)]
    other_side = (block_of(target) + blocks // 2) % blocks
    return jnp.where((block_of(source) == first) | (block_of(source) == other_side), factor * array, array)


def shard_levels(stream_key, dims, shards, least, top_value):
    loudness, own = 1.0, jax.random.fold_in(stream_key, 6)
    for dim, parts in shards:
        draws = jnp.exp(jax.random.uniform(jax.random.fold_in(own, dim), (parts,), jnp.float32, least / len(shards), top_value / len(shards)))
        loudness = loudness * jnp.repeat(draws, dims[dim] // parts).reshape([-1 if axis == dim else 1 for axis in range(len(dims))])
    return loudness


def length_profile(number_of, total, limit, slope):
    portions = [(1 << 20) // math.isqrt(rank ** slope) + 1 for rank in range(2, number_of + 1)]
    rest, holding = total - limit - (number_of - 1), [1] * (number_of - 1)
    while rest > 0:
        candidates = [i for i in range(number_of - 1) if holding[i] < limit]
        whole, left = sum([portions[i] for i in candidates]), rest
        for i in candidates:
            extra = min(limit - holding[i], max(1, left * portions[i] // whole), rest)
            holding[i] = holding[i] + extra
            rest = rest - extra
    return np.array([limit] + holding)


def ragged_sizes(rng, number_of, total, most, lean):
    if number_of == 2:
        one = jax.random.randint(rng, (), max(1, total - most), min(most, total - 1) + 1)
        return jnp.stack([one, total - one])
    sizes = jnp.asarray(length_profile(number_of, total, most, lean), jnp.int32)
    pairs = (number_of - 1) // 2
    giver, sink = sizes[1:1 + 2 * pairs:2], sizes[2:2 + 2 * pairs:2]
    slack = jnp.minimum(giver - 1, most - sink)
    shifted = jax.random.randint(jax.random.fold_in(rng, 1), (pairs,), 0, 1 << 20) % (slack + 1)
    sizes = sizes.at[1:1 + 2 * pairs:2].set(giver - shifted).at[2:2 + 2 * pairs:2].set(sink + shifted)
    return sizes[jax.random.permutation(jax.random.fold_in(rng, 2), number_of)]


def noise(stream_key, extent, width, reach, shards=(), held_as=jnp.bfloat16):
    values = width * jax.random.normal(stream_key, extent, jnp.float32)
    if shards:
        values = values * shard_levels(stream_key, extent, shards, -0.22, 0.18)
    return jnp.clip(values, -reach, reach).astype(held_as)


def gaussian_with(own_key, dims, width, reach, shards, heavy, held_as=jnp.bfloat16):
    array = width * jax.random.normal(own_key, dims, jnp.float32)
    if shards:
        array = array * shard_levels(own_key, dims, shards, -0.22, 0.18)
    return jnp.clip(with_spikes(array, jax.random.fold_in(own_key, 3), *heavy), -reach, reach).astype(held_as)


def setup_inputs(seed: int = 0) -> dict:
    key_of = jax.random.split(jax.random.key(seed), 21)
    return {
        "tokens": noise(key_of[0], (ROWS, SEQ_LEN, D), 1.0, 6.0, ((0, 16), (1, 2))),
        "prev_logits": noise(key_of[1], (ROWS, H, SEQ_LEN, SEQ_LEN), 1.0, 6.0, ((0, 16), (2, 2))),
        "segment_ids": jax.vmap(lambda own: jnp.searchsorted(jnp.cumsum(ragged_sizes(own, 6, SEQ_LEN, SEQ_LEN * 3 // 8, 0)), jnp.arange(SEQ_LEN), side="right"))(jax.random.split(key_of[2], ROWS)).reshape((ROWS, SEQ_LEN)).astype(jnp.int32),
        "out_cotangent": gaussian_with(key_of[3], (ROWS, SEQ_LEN, D), 1.0, 6.0, ((0, 16), (1, 2)), (0, 2, 16, 2.0)),
        "logit_cotangent": noise(key_of[4], (ROWS, H, SEQ_LEN, SEQ_LEN), 0.1, 0.59765625, ((0, 16), (2, 2))),
        "querymap": noise(key_of[5], (D, D), D ** -0.5, 0.21875, ((0, 32),)),
        "querybias": noise(key_of[6], (D,), 0.5, 3.0, ((0, 32),)),
        "keymap": noise(key_of[7], (D, D), D ** -0.5, 0.21875, ((0, 32),)),
        "valuemap": noise(key_of[8], (D, D), D ** -0.5, 0.21875, ((0, 32),)),
        "valuebias": noise(key_of[9], (D,), 0.5, 3.0, ((0, 32),)),
        "mixmap": noise(key_of[10], (D, D), (D // 64) ** -0.5, 1.75, ((0, 32),)),
        "mixbias": noise(key_of[11], (D,), 0.5, 3.0, ((0, 32),)),
        "normgain": jnp.clip(1.0 + 0.1 * jax.random.normal(key_of[12], (D,), jnp.float32), 0.5, 1.5).astype(jnp.bfloat16),
        "normbias": noise(key_of[13], (D,), 0.5, 3.0, ((0, 32),)),
        "expandmap": noise(key_of[14], (D, FF), D ** -0.5, 0.21875, ((0, 32),)),
        "expandbias": noise(key_of[15], (FF,), 0.5, 3.0, ((0, 32),)),
        "shrinkmap": noise(key_of[16], (FF, D), FF ** -0.5, 0.109375, ((0, 32),)),
        "shrinkbias": noise(key_of[17], (D,), 0.5, 3.0, ((0, 32),)),
        "outgain": jnp.clip(1.0 + 0.1 * jax.random.normal(key_of[18], (D,), jnp.float32), 0.5, 1.5).astype(jnp.bfloat16),
        "outbias": noise(key_of[19], (D,), 0.5, 3.0, ((0, 32),)),
    }


@jax.custom_vjp
def low(v):
    return lax.optimization_barrier(v.astype(jnp.bfloat16)).astype(jnp.float32)

@jax.custom_vjp
def low_back(v):
    return v

def low_keep(v):
    return (low(v), None)

def low_pass(kept, grad):
    return (grad,)

def back_keep(v):
    return (v, None)

def back_low(kept, grad):
    return (low(grad),)
low.defvjp(low_keep, low_pass)
low_back.defvjp(back_keep, back_low)
norm_eps = 1e-06
mask_fill = -1e+30
highest = lax.Precision.HIGHEST

def rounded(value):
    return low_back(low(value))

def matmul(left_side, right_side):
    return jnp.matmul(left_side, right_side, precision=highest)

def normalize(hidden, gain_row, shift_row):
    center = hidden - lax.optimization_barrier(jnp.mean(hidden, -1, keepdims=True))
    scaled = lax.rsqrt(lax.optimization_barrier(jnp.mean(center * center, -1, keepdims=True)) + norm_eps)
    return center * scaled * gain_row + shift_row

def forward(params, tokens, earlier, same_segment):
    querymap, querybias, keymap, valuemap, valuebias, mixmap, mixbias, normgain, normbias, expandmap, expandbias, shrinkmap, shrinkbias, outgain, outbias = params
    groups = tokens.shape[0]

    def split_heads(matrix):
        return matrix.reshape(groups, SEQ_LEN, H, HD)
    queries = rounded(matmul(tokens, querymap) + querybias)
    keys_all = rounded(matmul(tokens, keymap))
    values_all = rounded(matmul(tokens, valuemap) + valuebias)
    scores = jnp.einsum('gqhe,gkhe->ghqk', split_heads(queries), split_heads(keys_all), precision=highest)
    logits = low_back(earlier + scores * HD ** (-0.5))
    masked = jnp.where(same_segment, logits, mask_fill)
    row_peak = lax.optimization_barrier(jnp.max(masked, -1, keepdims=True))
    exponent = jnp.exp(masked - row_peak)
    attention = exponent / lax.optimization_barrier(jnp.sum(exponent, -1, keepdims=True))
    context = jnp.einsum('ghqk,gkhe->gqhe', low(attention), split_heads(values_all), precision=highest)
    context = rounded(context.reshape(groups, SEQ_LEN, H * HD))
    attended = low_back(matmul(context, mixmap) + mixbias)
    normed = low(normalize(tokens + attended, normgain, normbias))
    inner_pre = low_back(matmul(normed, expandmap) + expandbias)
    active = low(jax.nn.gelu(inner_pre, approximate=False))
    branch = low_back(matmul(active, shrinkmap) + shrinkbias)
    return (normalize(normed + branch, outgain, outbias), logits)

def reference(tokens, prev_logits, segment_ids, out_cotangent, logit_cotangent, querymap, querybias, keymap, valuemap, valuebias, mixmap, mixbias, normgain, normbias, expandmap, expandbias, shrinkmap, shrinkbias, outgain, outbias):
    params = tuple((weight.astype(jnp.float32) for weight in (querymap, querybias, keymap, valuemap, valuebias, mixmap, mixbias, normgain, normbias, expandmap, expandbias, shrinkmap, shrinkbias, outgain, outbias)))
    groups = math.gcd(ROWS, 4)
    blocks = ROWS // groups

    def one_block(totals, block_index):
        offset = (block_index * groups).astype(jnp.int32)

        def select(stack_item):
            return lax.dynamic_slice_in_dim(stack_item, offset, groups, 0)
        seg_block = select(segment_ids)
        same_segment = (seg_block[:, :, None] == seg_block[:, None, :])[:, None]

        def block_forward(weights, inputs, earlier):
            return forward(weights, inputs, earlier, same_segment)
        (output, logits), pullback = jax.vjp(block_forward, params, select(tokens).astype(jnp.float32), select(prev_logits).astype(jnp.float32))
        weight_grads, token_grad, earlier_grad = pullback((select(out_cotangent).astype(jnp.float32), select(logit_cotangent).astype(jnp.float32)))
        totals = tuple((running + increment for running, increment in zip(totals, weight_grads)))
        return (totals, (output.astype(jnp.bfloat16), logits.astype(jnp.bfloat16), token_grad.astype(jnp.bfloat16), earlier_grad.astype(jnp.bfloat16)))
    initial = tuple((jnp.zeros(weight.shape, jnp.float32) for weight in params))
    totals, stacked = lax.scan(one_block, initial, jnp.arange(blocks, dtype=jnp.int32))
    layer_out, raw_logits, tokens_grad, logits_grad = tuple((stack_item.reshape((ROWS,) + stack_item.shape[2:]) for stack_item in stacked))
    querymap_grad, querybias_grad, keymap_grad, valuemap_grad, valuebias_grad, mixmap_grad, mixbias_grad, normgain_grad, normbias_grad, expandmap_grad, expandbias_grad, shrinkmap_grad, shrinkbias_grad, outgain_grad, outbias_grad = totals
    return (layer_out, raw_logits, tokens_grad, logits_grad, querymap_grad, querybias_grad, keymap_grad, valuemap_grad, valuebias_grad, mixmap_grad, mixbias_grad, normgain_grad, normbias_grad, expandmap_grad, expandbias_grad, shrinkmap_grad, shrinkbias_grad, outgain_grad, outbias_grad)
```

```python
from functools import partial

import jax
import jax.numpy as jnp
from jax import lax
from jax.sharding import PartitionSpec as P

H = 12
HD = 64


norm_eps = 1e-06
mask_fill = -1e30


def matmul(left_side, right_side):
    return jnp.dot(left_side, right_side, preferred_element_type=jnp.float32)


def rows_product(left_side, right_side):
    return lax.dot_general(
        left_side, right_side, (((0,), (0,)), ((), ())), preferred_element_type=jnp.float32
    )


def cols_product(left_side, right_side):
    return lax.dot_general(
        left_side, right_side, (((1,), (1,)), ((), ())), preferred_element_type=jnp.float32
    )


def column_sum(matrix):
    return jnp.sum(matrix.astype(jnp.float32), 0)


def normalize(hidden):
    center = hidden - jnp.mean(hidden, -1, keepdims=True)
    scaled = lax.rsqrt(jnp.mean(center * center, -1, keepdims=True) + norm_eps)
    return (center * scaled, scaled)


def norm_back(upstream, unit_rows, scaled, gain_row):
    pulled = upstream * gain_row
    return scaled * (
        pulled
        - jnp.mean(pulled, -1, keepdims=True)
        - unit_rows * jnp.mean(pulled * unit_rows, -1, keepdims=True)
    )

AXES = ("dp", "seq")
VECTORS = (1, 4, 6, 7, 8, 10, 12, 13, 14)


def gather(block):
    return lax.all_gather(block, AXES, axis=0, tiled=False)


def body(tokens, prev_logits, segment_ids, out_cotangent, logit_cotangent, *shards):
    seqrows, qlength, width = tokens.shape
    klength = segment_ids.shape[1]
    factor = HD ** (-0.5)
    slots = seqrows * qlength
    devices = lax.axis_size(AXES)
    own_segment = lax.dynamic_slice_in_dim(segment_ids, lax.axis_index("seq") * qlength, qlength, 1)
    same_segment = (own_segment[:, :, None] == segment_ids[:, None, :])[:, None]
    (
        querymap, querybias, keymap, valuemap, valuebias, mixmap, mixbias, normgain, normbias,
        expandmap, expandbias, shrinkmap, shrinkbias, outgain, outbias,
    ) = shards
    own = querymap.shape[0]
    hidden = expandmap.shape[1]
    vectors = jnp.concatenate([shards[i] for i in VECTORS])
    vector_size = vectors.shape[0]
    vector_row = jnp.pad(vectors, (0, width - vector_size))[None]
    first_pack = gather(jnp.concatenate([querymap, keymap, valuemap, vector_row]))
    rest_pack = gather(jnp.concatenate([mixmap, shrinkmap, expandmap.reshape(-1, width)]))
    querymap, keymap, valuemap = [
        first_pack[:, i * own : (i + 1) * own].reshape(width, width) for i in range(3)
    ]
    vector_all = first_pack[:, 3 * own, :vector_size].astype(jnp.float32)
    sizes = [shards[i].shape[0] for i in VECTORS]
    parts, at = [], 0
    for size in sizes:
        parts.append(vector_all[:, at : at + size].reshape(-1))
        at += size
    querybias, valuebias, mixbias, normgain, normbias, expandbias, shrinkbias, outgain, outbias = parts
    wide = own * hidden // width
    mixmap = rest_pack[:, :own].reshape(width, width)
    shrinkmap = rest_pack[:, own : own + wide].reshape(hidden, width)
    expandmap = rest_pack[:, own + wide :].reshape(width, hidden)

    token_rows = tokens.reshape(slots, width)
    queries = (matmul(token_rows, querymap) + querybias).astype(jnp.bfloat16)
    keys_local = matmul(token_rows, keymap).astype(jnp.bfloat16)
    values_local = (matmul(token_rows, valuemap) + valuebias).astype(jnp.bfloat16)
    both = lax.all_gather(
        jnp.stack([keys_local, values_local]).reshape(2, seqrows, qlength, width), "seq", axis=2, tiled=True
    )
    query_heads = queries.reshape(seqrows, qlength, H, HD)
    key_heads = both[0].reshape(seqrows, klength, H, HD)
    value_heads = both[1].reshape(seqrows, klength, H, HD)

    def attend(operands):
        query_one, key_one, value_one, prior_one, same_one = operands
        scores = jnp.einsum("qhe,khe->hqk", query_one, key_one, preferred_element_type=jnp.float32)
        logits = prior_one.astype(jnp.float32) + scores * factor
        masked = jnp.where(same_one, logits, mask_fill)
        row_peak = jnp.max(masked, -1, keepdims=True)
        exponent = jnp.exp(masked - row_peak)
        attention = (exponent / jnp.sum(exponent, -1, keepdims=True)).astype(jnp.bfloat16)
        context = jnp.einsum("hqk,khe->qhe", attention, value_one, preferred_element_type=jnp.float32)
        return logits.astype(jnp.bfloat16), context.astype(jnp.bfloat16), attention

    raw_logits, context, attention_all = lax.map(
        attend, (query_heads, key_heads, value_heads, prev_logits, same_segment)
    )
    context = context.reshape(slots, width)
    attended = matmul(context, mixmap) + mixbias
    unit_first, scale_first = normalize(token_rows.astype(jnp.float32) + attended)
    normed = (unit_first * normgain + normbias).astype(jnp.bfloat16)
    inner_pre = matmul(normed, expandmap) + expandbias
    active, gelu_slope = jax.jvp(
        partial(jax.nn.gelu, approximate=False), (inner_pre,), (jnp.ones_like(inner_pre),)
    )
    active = active.astype(jnp.bfloat16)
    gelu_slope = gelu_slope.astype(jnp.bfloat16)
    second = normed.astype(jnp.float32) + (matmul(active, shrinkmap) + shrinkbias)
    unit_second, scale_second = normalize(second)
    layer_out = unit_second * outgain + outbias

    upstream = out_cotangent.reshape(slots, width).astype(jnp.float32)
    outgain_grad = jnp.sum(upstream * unit_second, 0)
    outbias_grad = jnp.sum(upstream, 0)
    second_grad = norm_back(upstream, unit_second, scale_second, outgain)
    branch_grad = second_grad.astype(jnp.bfloat16)
    shrinkbias_grad = column_sum(branch_grad)
    shrinkmap_grad = rows_product(active, branch_grad)
    active_grad = cols_product(branch_grad, shrinkmap)
    inner_grad = (active_grad * gelu_slope.astype(jnp.float32)).astype(jnp.bfloat16)
    expandbias_grad = column_sum(inner_grad)
    expandmap_grad = rows_product(normed, inner_grad)
    early = lax.psum_scatter(
        jnp.concatenate(
            [
                shrinkmap_grad.astype(jnp.bfloat16).reshape(devices, wide, width),
                expandmap_grad.astype(jnp.bfloat16).reshape(devices, wide, width),
            ],
            1,
        ),
        AXES,
        scatter_dimension=0,
        tiled=False,
    ).astype(jnp.float32)
    normed_grad = second_grad + cols_product(inner_grad, expandmap)
    normgain_grad = jnp.sum(normed_grad * unit_first, 0)
    normbias_grad = jnp.sum(normed_grad, 0)
    first_grad = norm_back(normed_grad, unit_first, scale_first, normgain)
    attended_grad = first_grad.astype(jnp.bfloat16)
    mixbias_grad = column_sum(attended_grad)
    mixmap_grad = rows_product(context, attended_grad)
    context_grad = cols_product(attended_grad, mixmap).astype(jnp.bfloat16).reshape(seqrows, qlength, H, HD)

    def attend_back(operands):
        query_one, key_one, value_one, attention_one, upstream_one, cotangent_one = operands
        attention = attention_one.astype(jnp.float32)
        prob_grad = jnp.einsum("qhe,khe->hqk", upstream_one, value_one, preferred_element_type=jnp.float32)
        row_dot = jnp.sum(prob_grad * attention, -1, keepdims=True)
        logit_grad = (cotangent_one.astype(jnp.float32) + attention * (prob_grad - row_dot)).astype(jnp.bfloat16)
        query_part = jnp.einsum("hqk,khe->qhe", logit_grad, key_one, preferred_element_type=jnp.float32) * factor
        key_part = jnp.einsum("hqk,qhe->khe", logit_grad, query_one, preferred_element_type=jnp.float32) * factor
        value_part = jnp.einsum("hqk,qhe->khe", attention_one, upstream_one, preferred_element_type=jnp.float32)
        return logit_grad, query_part.astype(jnp.bfloat16), jnp.stack([key_part, value_part]).astype(jnp.bfloat16)

    logits_grad, query_grad, both_partial = lax.map(
        attend_back, (query_heads, key_heads, value_heads, attention_all, context_grad, logit_cotangent)
    )
    both_grad = lax.psum_scatter(
        both_partial.reshape(seqrows, 2, klength, width), "seq", scatter_dimension=2, tiled=True
    )
    query_grad = query_grad.reshape(slots, width)
    key_grad = both_grad[:, 0].reshape(slots, width)
    value_grad = both_grad[:, 1].reshape(slots, width)
    querymap_grad = rows_product(token_rows, query_grad)
    querybias_grad = column_sum(query_grad)
    keymap_grad = rows_product(token_rows, key_grad)
    valuemap_grad = rows_product(token_rows, value_grad)
    valuebias_grad = column_sum(value_grad)
    tokens_grad = (
        first_grad
        + cols_product(query_grad, querymap)
        + cols_product(key_grad, keymap)
        + cols_product(value_grad, valuemap)
    )
    vector_grads = jnp.concatenate(
        [
            grad.reshape(devices, -1)
            for grad in (
                querybias_grad, valuebias_grad, mixbias_grad, normgain_grad, normbias_grad,
                expandbias_grad, shrinkbias_grad, outgain_grad, outbias_grad,
            )
        ],
        1,
    )
    vector_grads = jnp.pad(vector_grads, ((0, 0), (0, width - vector_size)))[:, None]
    late = lax.psum_scatter(
        jnp.concatenate(
            [
                querymap_grad.reshape(devices, own, width),
                keymap_grad.reshape(devices, own, width),
                valuemap_grad.reshape(devices, own, width),
                mixmap_grad.reshape(devices, own, width),
                vector_grads,
            ],
            1,
        ).astype(jnp.bfloat16),
        AXES,
        scatter_dimension=0,
        tiled=False,
    ).astype(jnp.float32)
    vector_own, parts, at = late[4 * own], [], 0
    for size in sizes:
        parts.append(vector_own[at : at + size])
        at += size
    (
        querybias_grad, valuebias_grad, mixbias_grad, normgain_grad, normbias_grad,
        expandbias_grad, shrinkbias_grad, outgain_grad, outbias_grad,
    ) = parts
    owned = (
        late[:own], querybias_grad, late[own : 2 * own], late[2 * own : 3 * own], valuebias_grad,
        late[3 * own : 4 * own], mixbias_grad, normgain_grad, normbias_grad,
        early[wide:].reshape(own, hidden), expandbias_grad, early[:wide], shrinkbias_grad,
        outgain_grad, outbias_grad,
    )
    return (
        layer_out.reshape(seqrows, qlength, width).astype(jnp.bfloat16),
        raw_logits,
        tokens_grad.reshape(seqrows, qlength, width).astype(jnp.bfloat16),
        logits_grad,
    ) + owned


def solution(mesh):
    in_specs = (
        P("dp", "seq", None),
        P("dp", None, "seq", None),
        P("dp", None),
        P("dp", "seq", None),
        P("dp", None, "seq", None),
        P(("dp", "seq"), None),
        P(("dp", "seq")),
        P(("dp", "seq"), None),
        P(("dp", "seq"), None),
        P(("dp", "seq")),
        P(("dp", "seq"), None),
        P(("dp", "seq")),
        P(("dp", "seq")),
        P(("dp", "seq")),
        P(("dp", "seq"), None),
        P(("dp", "seq")),
        P(("dp", "seq"), None),
        P(("dp", "seq")),
        P(("dp", "seq")),
        P(("dp", "seq")),
    )
    out_specs = (
        P("dp", "seq", None),
        P("dp", None, "seq", None),
        P("dp", "seq", None),
        P("dp", None, "seq", None),
        P(("dp", "seq"), None),
        P(("dp", "seq")),
        P(("dp", "seq"), None),
        P(("dp", "seq"), None),
        P(("dp", "seq")),
        P(("dp", "seq"), None),
        P(("dp", "seq")),
        P(("dp", "seq")),
        P(("dp", "seq")),
        P(("dp", "seq"), None),
        P(("dp", "seq")),
        P(("dp", "seq"), None),
        P(("dp", "seq")),
        P(("dp", "seq")),
        P(("dp", "seq")),
    )
    return jax.shard_map(body, mesh=mesh, in_specs=in_specs, out_specs=out_specs, check_vma=False)
```

```python
from functools import partial

import jax
import jax.numpy as jnp
from jax import lax
from jax.experimental import pallas as pl
from jax.experimental.pallas import tpu as pltpu
from jax.sharding import PartitionSpec as P

H = 12
HD = 64
PAIR = 2 * HD
MESH = pl.DeviceIdType.MESH
ANY = pl.BlockSpec(memory_space=pl.ANY)
VMEM = pl.BlockSpec(memory_space=pltpu.VMEM)


norm_eps = 1e-06
mask_fill = -1e30


def matmul(left_side, right_side):
    return jnp.dot(left_side, right_side, preferred_element_type=jnp.float32)


def rows_product(left_side, right_side):
    return lax.dot_general(
        left_side, right_side, (((0,), (0,)), ((), ())), preferred_element_type=jnp.float32
    )


def cols_product(left_side, right_side):
    return lax.dot_general(
        left_side, right_side, (((1,), (1,)), ((), ())), preferred_element_type=jnp.float32
    )


def column_sum(matrix):
    return jnp.sum(matrix.astype(jnp.float32), 0)


def normalize(hidden):
    center = hidden - jnp.mean(hidden, -1, keepdims=True)
    scaled = lax.rsqrt(jnp.mean(center * center, -1, keepdims=True) + norm_eps)
    return (center * scaled, scaled)


def norm_back(upstream, unit_rows, scaled, gain_row):
    pulled = upstream * gain_row
    return scaled * (
        pulled
        - jnp.mean(pulled, -1, keepdims=True)
        - unit_rows * jnp.mean(pulled * unit_rows, -1, keepdims=True)
    )


def flip(index, bit):
    return index + bit * (1 - 2 * lax.rem(index // bit, 2))


def flip_mask(index, mask):
    bit = 1
    while bit <= mask:
        if mask & bit:
            index = flip(index, bit)
        bit *= 2
    return index


def masks_of(order):
    masks = [0]
    for place in order:
        masks = masks + [mask ^ (1 << place) for mask in masks]
    return masks


def orders_of(bits):
    first = list(range(bits - 1, -1, -1))
    second = list(first)
    if bits >= 2:
        second[-1], second[-2] = second[-2], second[-1]
    return first, second


def barrier(bits, me, core):
    gate = pltpu.get_barrier_semaphore()
    for place in range(bits):
        pl.semaphore_signal(gate, inc=1, device_id=(flip(me, 1 << place), core), device_id_type=MESH)
    pl.semaphore_signal(gate, inc=1, device_id=(me, 1 - core), device_id_type=MESH)
    pl.semaphore_wait(gate, bits + 1)


def wait_bytes(region, semaphore):
    pltpu.make_async_copy(region, region, semaphore).wait()


class Gather:
    def __init__(self, bits, shards, fulls, hop_sems, core_sems, send_sems, own_sems):
        self.bits, self.shards, self.fulls = bits, shards, fulls
        self.hop_sems, self.core_sems = hop_sems, core_sems
        self.send_sems, self.own_sems = send_sems, own_sems
        self.orders = [orders_of(bits)[i % 2] for i in range(len(shards))]
        self.me, self.core = lax.axis_index("dp"), lax.axis_index("seq")

    def slot(self, mask):
        return flip_mask(self.me, mask) * 2 + self.core

    def own(self, i):
        return pltpu.make_async_copy(self.shards[i], self.fulls[i].at[self.slot(0)], self.own_sems.at[i])

    def send(self, i, mask, device, semaphore):
        slot = self.slot(mask)
        source = self.fulls[i].at[slot] if mask else self.shards[i]
        pltpu.make_async_remote_copy(
            src_ref=source, dst_ref=self.fulls[i].at[slot], send_sem=self.send_sems.at[i],
            recv_sem=semaphore, device_id=device, device_id_type=MESH,
        ).start()

    def phase(self, step):
        for i in range(len(self.shards)):
            masks = masks_of(self.orders[i])
            fresh = masks[:1] if step == 0 else masks[1 << (step - 1) : 1 << step]
            if step == 0:
                self.own(i).start()
            else:
                wait_bytes(self.fulls[i].at[pl.ds(0, len(fresh))], self.hop_sems.at[i, step - 1])
            if step < self.bits:
                partner = (flip(self.me, 1 << self.orders[i][step]), self.core)
                for mask in masks[: 1 << step]:
                    self.send(i, mask, partner, self.hop_sems.at[i, step])
            for mask in fresh:
                self.send(i, mask, (self.me, 1 - self.core), self.core_sems.at[i])

    def finish(self):
        size = 1 << self.bits
        for i in range(len(self.shards)):
            wait_bytes(self.fulls[i].at[pl.ds(0, size)], self.core_sems.at[i])
            wait_bytes(self.fulls[i].at[pl.ds(0, 2 * size - 1)], self.send_sems.at[i])
            self.own(i).wait()

    def phases(self):
        return [partial(self.phase, step) for step in range(self.bits + 1)] + [self.finish]


def gather_scratch(count, bits):
    return [
        pltpu.SemaphoreType.DMA((count, bits)),
        pltpu.SemaphoreType.DMA((count,)),
        pltpu.SemaphoreType.DMA((count,)),
        pltpu.SemaphoreType.DMA((count,)),
    ]


def gather_kernel(bits, count, tokens_ref, *refs):
    shards, (both_ref, *fulls) = refs[:count], refs[count : 2 * count + 1]
    sems = refs[2 * count + 1 : 2 * count + 5]
    token_sems = refs[2 * count + 5]
    me, core = lax.axis_index("dp"), lax.axis_index("seq")
    barrier(bits, me, core)
    gather = Gather(bits, shards, fulls, *sems)
    phases = gather.phases()
    phases[0]()
    mine = pltpu.make_async_copy(tokens_ref, both_ref.at[0], token_sems.at[0])
    other = pltpu.make_async_remote_copy(
        src_ref=tokens_ref, dst_ref=both_ref.at[1], send_sem=token_sems.at[1], recv_sem=token_sems.at[2],
        device_id=(me, 1 - core), device_id_type=MESH,
    )
    mine.start()
    other.start()
    for phase in phases[1:]:
        phase()
    mine.wait()
    other.wait()


def gather_all(bits, tokens, shards):
    count, devices = len(shards), 2 << bits
    outs = [jax.ShapeDtypeStruct((2,) + tokens.shape, tokens.dtype)]
    outs += [jax.ShapeDtypeStruct((devices,) + shard.shape, shard.dtype) for shard in shards]
    return pl.pallas_call(
        partial(gather_kernel, bits, count),
        out_shape=outs,
        in_specs=[VMEM] * (count + 1),
        out_specs=[ANY] * (count + 1),
        scratch_shapes=gather_scratch(count, bits) + [pltpu.SemaphoreType.DMA((3,))],
        compiler_params=pltpu.CompilerParams(collective_id=0, has_side_effects=True),
        name="gather_all",
    )(tokens, *shards)


class Scatter:
    def __init__(self, bits, grads, outs, locals_, boxes, box_sems, load_sems, send_sems):
        self.bits, self.grads, self.outs, self.locals, self.boxes = bits, grads, outs, locals_, boxes
        self.box_sems, self.load_sems, self.send_sems = box_sems, load_sems, send_sems
        self.orders = [orders_of(bits)[i % 2] for i in range(len(grads))]
        self.me, self.core = lax.axis_index("dp"), lax.axis_index("seq")

    def start(self):
        size = 1 << self.bits
        half = size // 2
        for part in (1, 0):
            for i, grad in enumerate(self.grads):
                masks = masks_of(self.orders[i])
                for place in range(part * half, part * half + half):
                    device = flip_mask(self.me, masks[place])
                    pltpu.make_async_remote_copy(
                        src_ref=grad.at[device * 2 + 1 - self.core], dst_ref=self.boxes[i].at[place],
                        send_sem=self.send_sems.at[i], recv_sem=self.box_sems.at[i, part],
                        device_id=(self.me, 1 - self.core), device_id_type=MESH,
                    ).start()
                    pltpu.make_async_copy(
                        grad.at[device * 2 + self.core], self.locals[i].at[place], self.load_sems.at[i, part]
                    ).start()

    def add(self, i, base, other_ref, other_base, count):
        box = self.boxes[i]

        def one(place, carry):
            total = box[base + place].astype(jnp.float32) + other_ref[other_base + place].astype(jnp.float32)
            box[base + place] = total.astype(jnp.bfloat16)
            return carry

        lax.fori_loop(0, count, one, 0)

    def base(self, step):
        at = 0
        for later in range(self.bits, step, -1):
            at += 1 << later
        return at

    def send(self, i, step):
        count = 1 << step
        pltpu.make_async_remote_copy(
            src_ref=self.boxes[i].at[pl.ds(self.base(step + 1) + count, count)],
            dst_ref=self.boxes[i].at[pl.ds(self.base(step), count)],
            send_sem=self.send_sems.at[i], recv_sem=self.box_sems.at[i, 2 + step],
            device_id=(flip(self.me, 1 << self.orders[i][step]), self.core), device_id_type=MESH,
        ).start()

    def halves(self, part):
        half = 1 << (self.bits - 1)
        for i in range(len(self.grads)):
            wait_bytes(self.locals[i].at[pl.ds(0, half)], self.load_sems.at[i, part])
            wait_bytes(self.boxes[i].at[pl.ds(0, half)], self.box_sems.at[i, part])
            self.add(i, part * half, self.locals[i], part * half, half)
            if part:
                self.send(i, self.bits - 1)

    def step(self, step):
        count = 1 << step
        for i in range(len(self.grads)):
            at, kept = self.base(step), self.base(step + 1)
            wait_bytes(self.boxes[i].at[pl.ds(at, count)], self.box_sems.at[i, 2 + step])
            if step:
                half = count // 2
                self.add(i, at + half, self.boxes[i], kept + half, half)
                self.send(i, step - 1)
                self.add(i, at, self.boxes[i], kept, half)
            else:
                self.outs[i][...] = self.boxes[i][at].astype(jnp.float32) + self.boxes[i][kept].astype(jnp.float32)

    def finish(self):
        total = (2 << self.bits) - 1
        for i in range(len(self.grads)):
            wait_bytes(self.boxes[i].at[pl.ds(0, total)], self.send_sems.at[i])

    def phases(self):
        return (
            [self.start, partial(self.halves, 1), partial(self.halves, 0)]
            + [partial(self.step, step) for step in range(self.bits - 1, -1, -1)]
            + [self.finish]
        )


def scatter_scratch(grads, bits):
    size = 1 << bits
    return (
        [pltpu.VMEM((size,) + grad.shape[1:], jnp.bfloat16) for grad in grads]
        + [pltpu.VMEM((2 * size - 1,) + grad.shape[1:], jnp.bfloat16) for grad in grads]
        + [
            pltpu.SemaphoreType.DMA((len(grads), bits + 2)),
            pltpu.SemaphoreType.DMA((len(grads), 2)),
            pltpu.SemaphoreType.DMA((len(grads),)),
        ]
    )


def scatter_kernel(bits, count, partial_ref, *refs):
    grads, (other_ref, *outs) = refs[:count], refs[count : 2 * count + 1]
    rest = refs[2 * count + 1 :]
    locals_, boxes, sems, swap_sems = rest[:count], rest[count : 2 * count], rest[2 * count : 2 * count + 3], rest[-1]
    me, core = lax.axis_index("dp"), lax.axis_index("seq")
    barrier(bits, me, core)
    scatter = Scatter(bits, grads, outs, locals_, boxes, *sems)
    phases = scatter.phases()
    phases[0]()
    swap = pltpu.make_async_remote_copy(
        src_ref=partial_ref, dst_ref=other_ref, send_sem=swap_sems.at[0], recv_sem=swap_sems.at[1],
        device_id=(me, 1 - core), device_id_type=MESH,
    )
    swap.start()
    for phase in phases[1:]:
        phase()
    swap.wait()


def scatter_all(bits, swapped, grads):
    count = len(grads)
    outs = [jax.ShapeDtypeStruct(swapped.shape, swapped.dtype)]
    outs += [jax.ShapeDtypeStruct(grad.shape[1:], jnp.float32) for grad in grads]
    return pl.pallas_call(
        partial(scatter_kernel, bits, count),
        out_shape=outs,
        in_specs=[ANY] * (count + 1),
        out_specs=[ANY] + [VMEM] * count,
        scratch_shapes=scatter_scratch(grads, bits) + [pltpu.SemaphoreType.DMA((2,))],
        compiler_params=pltpu.CompilerParams(
            collective_id=1, has_side_effects=True, vmem_limit_bytes=58 * 2**20
        ),
        name="scatter_all",
    )(swapped, *grads)


def lane_mask(rows, head):
    lanes = lax.broadcasted_iota(jnp.int32, (rows, PAIR), 1)
    return (lanes // HD) == head


def only(matrix, head):
    return jnp.where(lane_mask(matrix.shape[0], head), matrix, jnp.zeros_like(matrix))


def join_halves(pair_ref, whole_ref, core):
    half = pair_ref.shape[2]
    whole_ref[pl.ds(pl.multiple_of(core * half, half), half)] = pair_ref[0, 0]
    whole_ref[pl.ds(pl.multiple_of((1 - core) * half, half), half)] = pair_ref[1, 0]


def attend_kernel(
    q_ref, k_ref, v_ref, prior_ref, own_ref, all_ref, logits_ref, context_ref, probs_ref, key_ref, value_ref, score_ref
):
    core = lax.axis_index("seq")
    join_halves(k_ref, key_ref, core)
    join_halves(v_ref, value_ref, core)
    rows = q_ref.shape[1]
    chunk = 64
    query = q_ref[0] * jnp.bfloat16(HD ** (-0.5))
    for head in range(2):
        score_ref[head] = cols_product(only(query, head), key_ref[...])
    for start in range(0, rows, chunk):
        same = own_ref[0, pl.ds(start, chunk)] == all_ref[0]
        for head in range(2):
            logits = prior_ref[0, head, pl.ds(start, chunk)].astype(jnp.float32) + score_ref[head, pl.ds(start, chunk)]
            logits_ref[0, head, pl.ds(start, chunk)] = logits.astype(jnp.bfloat16)
            masked = jnp.where(same, logits, mask_fill)
            exponent = jnp.exp(masked - jnp.max(masked, -1, keepdims=True))
            weight = 1.0 / jnp.sum(exponent, -1, keepdims=True)
            probs_ref[0, head, pl.ds(start, chunk)] = (exponent * weight).astype(jnp.bfloat16)
    value = value_ref[...]
    context = matmul(probs_ref[0, 0], only(value, 0)) + matmul(probs_ref[0, 1], only(value, 1))
    context_ref[0] = context.astype(jnp.bfloat16)


def attend(queries, keys, values, prev_logits, own_segment, segment_ids):
    rows, qlength, width = queries.shape
    klength = segment_ids.shape[1]
    rect = pl.BlockSpec((1, 2, qlength, klength), lambda r, p: (r, p, 0, 0))
    slim = pl.BlockSpec((1, qlength, PAIR), lambda r, p: (r, 0, p))
    pair = pl.BlockSpec((2, 1, qlength, PAIR), lambda r, p: (0, r, 0, p))
    return pl.pallas_call(
        attend_kernel,
        grid=(rows, width // PAIR),
        out_shape=[
            jax.ShapeDtypeStruct(prev_logits.shape, jnp.bfloat16),
            jax.ShapeDtypeStruct(queries.shape, jnp.bfloat16),
            jax.ShapeDtypeStruct(prev_logits.shape, jnp.bfloat16),
        ],
        in_specs=[
            slim, pair, pair, rect,
            pl.BlockSpec((1, qlength, 1), lambda r, p: (r, 0, 0)),
            pl.BlockSpec((1, 1, klength), lambda r, p: (r, 0, 0)),
        ],
        out_specs=[rect, slim, rect],
        scratch_shapes=[
            pltpu.VMEM((klength, PAIR), jnp.bfloat16),
            pltpu.VMEM((klength, PAIR), jnp.bfloat16),
            pltpu.VMEM((2, qlength, klength), jnp.float32),
        ],
        compiler_params=pltpu.CompilerParams(vmem_limit_bytes=32 * 2**20),
        name="attend",
    )(queries, keys, values, prev_logits, own_segment[:, :, None], segment_ids[:, None, :])


def attend_back_kernel(
    q_ref, k_ref, v_ref, probs_ref, upstream_ref, context_ref, cotangent_ref,
    logit_grad_ref, query_grad_ref, key_grad_ref, value_grad_ref, key_ref, value_ref, score_ref, turn_ref,
):
    core = lax.axis_index("seq")
    join_halves(k_ref, key_ref, core)
    join_halves(v_ref, value_ref, core)
    rows = q_ref.shape[1]
    chunk = 64
    factor = HD ** (-0.5)
    upstream = upstream_ref[0]
    products = upstream.astype(jnp.float32) * context_ref[0].astype(jnp.float32)
    for head in range(2):
        score_ref[head] = cols_product(only(upstream, head), value_ref[...])
    for head in range(2):
        row_dot = jnp.sum(only(products, head), -1, keepdims=True)
        for start in range(0, rows, chunk):
            span = pl.ds(start, chunk)
            probs = probs_ref[0, head, span].astype(jnp.float32)
            grad = cotangent_ref[0, head, span].astype(jnp.float32) + probs * (
                score_ref[head, span] - row_dot[start : start + chunk]
            )
            logit_grad_ref[0, head, span] = grad.astype(jnp.bfloat16)
    key = key_ref[...]
    query_grad = matmul(logit_grad_ref[0, 0], only(key, 0)) + matmul(logit_grad_ref[0, 1], only(key, 1))
    query_grad_ref[0] = (query_grad * factor).astype(jnp.bfloat16)
    query_turned = (q_ref[0].astype(jnp.float32) * factor).T.astype(jnp.bfloat16)
    upstream_turned = upstream.astype(jnp.float32).T.astype(jnp.bfloat16)
    half = key_grad_ref.shape[2]
    for left, right_ref, out_ref in (
        (query_turned, logit_grad_ref, key_grad_ref),
        (upstream_turned, probs_ref, value_grad_ref),
    ):
        for head in range(2):
            turn_ref[head * HD : (head + 1) * HD] = matmul(left[head * HD : (head + 1) * HD], right_ref[0, head])
        score_ref[0, :, :PAIR] = turn_ref[:, :half].T
        score_ref[1, :, :PAIR] = turn_ref[:, half:].T
        out_ref[0, 0] = score_ref[core, :, :PAIR].astype(jnp.bfloat16)
        out_ref[1, 0] = score_ref[1 - core, :, :PAIR].astype(jnp.bfloat16)


def attend_back(queries, keys, values, probs, upstream, context, cotangent):
    rows, qlength, width = queries.shape
    klength = probs.shape[-1]
    rect = pl.BlockSpec((1, 2, qlength, klength), lambda r, p: (r, p, 0, 0))
    slim = pl.BlockSpec((1, qlength, PAIR), lambda r, p: (r, 0, p))
    pair = pl.BlockSpec((2, 1, qlength, PAIR), lambda r, p: (0, r, 0, p))
    return pl.pallas_call(
        attend_back_kernel,
        grid=(rows, width // PAIR),
        out_shape=[
            jax.ShapeDtypeStruct(cotangent.shape, jnp.bfloat16),
            jax.ShapeDtypeStruct(queries.shape, jnp.bfloat16),
            jax.ShapeDtypeStruct(keys.shape, jnp.bfloat16),
            jax.ShapeDtypeStruct(values.shape, jnp.bfloat16),
        ],
        in_specs=[slim, pair, pair, rect, slim, slim, rect],
        out_specs=[rect, slim, pair, pair],
        scratch_shapes=[
            pltpu.VMEM((klength, PAIR), jnp.bfloat16),
            pltpu.VMEM((klength, PAIR), jnp.bfloat16),
            pltpu.VMEM((2, qlength, klength), jnp.float32),
            pltpu.VMEM((PAIR, klength), jnp.float32),
        ],
        compiler_params=pltpu.CompilerParams(vmem_limit_bytes=32 * 2**20),
        name="attend_back",
    )(queries, keys, values, probs, upstream, context, cotangent)


LANES = 128


def pack_vectors(rows, wide):
    block = jnp.pad(jnp.stack(rows, -2), ((0, 0),) * (rows[0].ndim - 1) + ((0, 0), (0, LANES - rows[0].shape[-1])))
    long_row = jnp.pad(wide, ((0, 0),) * (wide.ndim - 1) + ((0, LANES - wide.shape[-1]),))[..., None, :]
    block = jnp.concatenate([block, long_row], -2)
    return jnp.pad(block, ((0, 0),) * (block.ndim - 2) + ((0, 16 - block.shape[-2]), (0, 0)))


def body(tokens, prev_logits, segment_ids, out_cotangent, logit_cotangent, *shards):
    seqrows, qlength, width = tokens.shape
    slots = seqrows * qlength
    chips = lax.axis_size("dp")
    bits = chips.bit_length() - 1
    devices = 2 * chips
    (
        querymap, querybias, keymap, valuemap, valuebias, mixmap, mixbias, normgain, normbias,
        expandmap, expandbias, shrinkmap, shrinkbias, outgain, outbias,
    ) = shards
    own = querymap.shape[0]
    hidden = expandmap.shape[1]
    wide = expandbias.shape[0]
    own_segment = lax.dynamic_slice_in_dim(segment_ids, lax.axis_index("seq") * qlength, qlength, 1)

    block = pack_vectors(
        [querybias, valuebias, mixbias, normgain, normbias, shrinkbias, outgain, outbias], expandbias
    )
    both_tokens, querymap, keymap, valuemap, block, mixmap, shrinkmap, expandmap = gather_all(
        bits, tokens, [querymap, keymap, valuemap, block, mixmap, shrinkmap, expandmap]
    )
    querymap, keymap, valuemap, mixmap = [m.reshape(width, width) for m in (querymap, keymap, valuemap, mixmap)]
    expandmap = expandmap.reshape(width, hidden)
    shrinkmap = shrinkmap.reshape(hidden, width)
    block = block.astype(jnp.float32)
    rows = block[:, :8, :own].transpose(1, 0, 2).reshape(8, width)
    querybias, valuebias, mixbias, normgain, normbias, shrinkbias, outgain, outbias = [rows[i] for i in range(8)]
    expandbias = block[:, 8, :wide].reshape(hidden)

    token_rows = tokens.reshape(slots, width)
    both_rows = both_tokens.reshape(2 * slots, width)
    queries = (matmul(token_rows, querymap) + querybias).astype(jnp.bfloat16).reshape(seqrows, qlength, width)
    keys = matmul(both_rows, keymap).astype(jnp.bfloat16).reshape(2, seqrows, qlength, width)
    values = (matmul(both_rows, valuemap) + valuebias).astype(jnp.bfloat16).reshape(2, seqrows, qlength, width)
    raw_logits, context_heads, probs = attend(queries, keys, values, prev_logits, own_segment, segment_ids)
    context = context_heads.reshape(slots, width)
    attended = matmul(context, mixmap) + mixbias
    unit_first, scale_first = normalize(token_rows.astype(jnp.float32) + attended)
    normed = (unit_first * normgain + normbias).astype(jnp.bfloat16)
    inner_pre = matmul(normed, expandmap) + expandbias
    active, gelu_slope = jax.jvp(
        partial(jax.nn.gelu, approximate=False), (inner_pre,), (jnp.ones_like(inner_pre),)
    )
    active = active.astype(jnp.bfloat16)
    gelu_slope = gelu_slope.astype(jnp.bfloat16)
    second = normed.astype(jnp.float32) + (matmul(active, shrinkmap) + shrinkbias)
    unit_second, scale_second = normalize(second)
    layer_out = unit_second * outgain + outbias

    upstream = out_cotangent.reshape(slots, width).astype(jnp.float32)
    outgain_grad = jnp.sum(upstream * unit_second, 0)
    outbias_grad = jnp.sum(upstream, 0)
    second_grad = norm_back(upstream, unit_second, scale_second, outgain)
    branch_grad = second_grad.astype(jnp.bfloat16)
    shrinkbias_grad = column_sum(branch_grad)
    shrinkmap_grad = rows_product(active, branch_grad).astype(jnp.bfloat16)
    active_grad = cols_product(branch_grad, shrinkmap)
    inner_grad = (active_grad * gelu_slope.astype(jnp.float32)).astype(jnp.bfloat16)
    expandbias_grad = column_sum(inner_grad)
    expandmap_grad = rows_product(normed, inner_grad).astype(jnp.bfloat16)
    normed_grad = second_grad + cols_product(inner_grad, expandmap)
    normgain_grad = jnp.sum(normed_grad * unit_first, 0)
    normbias_grad = jnp.sum(normed_grad, 0)
    first_grad = norm_back(normed_grad, unit_first, scale_first, normgain)
    attended_grad = first_grad.astype(jnp.bfloat16)
    mixbias_grad = column_sum(attended_grad)
    mixmap_grad = rows_product(context, attended_grad).astype(jnp.bfloat16)
    context_grad = cols_product(attended_grad, mixmap).astype(jnp.bfloat16).reshape(seqrows, qlength, width)
    logits_grad, query_grad, key_grad, value_grad = attend_back(
        queries, keys, values, probs, context_grad, context_heads, logit_cotangent
    )
    query_grad = query_grad.reshape(slots, width)
    key_grad = key_grad.reshape(2 * slots, width)
    value_grad = value_grad.reshape(2 * slots, width)
    other_grad = (
        cols_product(key_grad[slots:], keymap) + cols_product(value_grad[slots:], valuemap)
    ).astype(jnp.bfloat16)
    querymap_grad = rows_product(token_rows, query_grad).astype(jnp.bfloat16)
    querybias_grad = column_sum(query_grad)
    keymap_grad = rows_product(both_rows, key_grad).astype(jnp.bfloat16)
    valuemap_grad = rows_product(both_rows, value_grad).astype(jnp.bfloat16)
    valuebias_grad = column_sum(value_grad)
    tokens_grad = (
        first_grad
        + cols_product(query_grad, querymap)
        + cols_product(key_grad[:slots], keymap)
        + cols_product(value_grad[:slots], valuemap)
    )
    block = pack_vectors(
        [
            grad.reshape(devices, own)
            for grad in (
                querybias_grad, valuebias_grad, mixbias_grad, normgain_grad, normbias_grad,
                shrinkbias_grad, outgain_grad, outbias_grad,
            )
        ],
        expandbias_grad.reshape(devices, wide),
    ).astype(jnp.bfloat16)
    swapped, querymap_grad, keymap_grad, valuemap_grad, block, mixmap_grad, shrinkmap_grad, expandmap_grad = scatter_all(
        bits,
        other_grad,
        [
            querymap_grad.reshape(devices, own, width),
            keymap_grad.reshape(devices, own, width),
            valuemap_grad.reshape(devices, own, width),
            block,
            mixmap_grad.reshape(devices, own, width),
            shrinkmap_grad.reshape(devices, wide, width),
            expandmap_grad.reshape(devices, own, hidden),
        ],
    )
    tokens_grad = tokens_grad + swapped.astype(jnp.float32)
    (
        querybias_grad, valuebias_grad, mixbias_grad, normgain_grad, normbias_grad,
        shrinkbias_grad, outgain_grad, outbias_grad,
    ) = [block[i, :own] for i in range(8)]
    expandbias_grad = block[8, :wide]
    return (
        layer_out.reshape(seqrows, qlength, width).astype(jnp.bfloat16),
        raw_logits,
        tokens_grad.reshape(seqrows, qlength, width).astype(jnp.bfloat16),
        logits_grad,
        querymap_grad, querybias_grad, keymap_grad, valuemap_grad, valuebias_grad,
        mixmap_grad, mixbias_grad, normgain_grad, normbias_grad,
        expandmap_grad, expandbias_grad, shrinkmap_grad, shrinkbias_grad,
        outgain_grad, outbias_grad,
    )


def solution(mesh):
    in_specs = (
        P("dp", "seq", None),
        P("dp", None, "seq", None),
        P("dp", None),
        P("dp", "seq", None),
        P("dp", None, "seq", None),
        P(("dp", "seq"), None),
        P(("dp", "seq")),
        P(("dp", "seq"), None),
        P(("dp", "seq"), None),
        P(("dp", "seq")),
        P(("dp", "seq"), None),
        P(("dp", "seq")),
        P(("dp", "seq")),
        P(("dp", "seq")),
        P(("dp", "seq"), None),
        P(("dp", "seq")),
        P(("dp", "seq"), None),
        P(("dp", "seq")),
        P(("dp", "seq")),
        P(("dp", "seq")),
    )
    out_specs = (
        P("dp", "seq", None),
        P("dp", None, "seq", None),
        P("dp", "seq", None),
        P("dp", None, "seq", None),
        P(("dp", "seq"), None),
        P(("dp", "seq")),
        P(("dp", "seq"), None),
        P(("dp", "seq"), None),
        P(("dp", "seq")),
        P(("dp", "seq"), None),
        P(("dp", "seq")),
        P(("dp", "seq")),
        P(("dp", "seq")),
        P(("dp", "seq"), None),
        P(("dp", "seq")),
        P(("dp", "seq"), None),
        P(("dp", "seq")),
        P(("dp", "seq")),
        P(("dp", "seq")),
    )
    return jax.shard_map(body, mesh=mesh, in_specs=in_specs, out_specs=out_specs, check_vma=False)
```

```python
from functools import partial

import jax
import jax.numpy as jnp
from jax import lax
from jax.experimental import pallas as pl
from jax.experimental.pallas import tpu as pltpu
from jax.sharding import PartitionSpec as P

H = 12
HD = 64
PAIR = 2 * HD
MESH = pl.DeviceIdType.MESH
ANY = pl.BlockSpec(memory_space=pl.ANY)
VMEM = pl.BlockSpec(memory_space=pltpu.VMEM)


norm_eps = 1e-06
mask_fill = -1e30


def matmul(left_side, right_side):
    return jnp.dot(left_side, right_side, preferred_element_type=jnp.float32)


def rows_product(left_side, right_side):
    return lax.dot_general(
        left_side, right_side, (((0,), (0,)), ((), ())), preferred_element_type=jnp.float32
    )


def cols_product(left_side, right_side):
    return lax.dot_general(
        left_side, right_side, (((1,), (1,)), ((), ())), preferred_element_type=jnp.float32
    )


def column_sum(matrix):
    return jnp.sum(matrix.astype(jnp.float32), 0)


def normalize(hidden):
    center = hidden - jnp.mean(hidden, -1, keepdims=True)
    scaled = lax.rsqrt(jnp.mean(center * center, -1, keepdims=True) + norm_eps)
    return (center * scaled, scaled)


def norm_back(upstream, unit_rows, scaled, gain_row):
    pulled = upstream * gain_row
    return scaled * (
        pulled
        - jnp.mean(pulled, -1, keepdims=True)
        - unit_rows * jnp.mean(pulled * unit_rows, -1, keepdims=True)
    )


def flip(index, bit):
    return index + bit * (1 - 2 * lax.rem(index // bit, 2))


def flip_mask(index, mask):
    bit = 1
    while bit <= mask:
        if mask & bit:
            index = flip(index, bit)
        bit *= 2
    return index


def masks_of(order):
    masks = [0]
    for place in order:
        masks = masks + [mask ^ (1 << place) for mask in masks]
    return masks


def orders_of(bits):
    first = list(range(bits - 1, -1, -1))
    second = list(first)
    if bits >= 2:
        second[-1], second[-2] = second[-2], second[-1]
    return first, second


def barrier(bits, me, core):
    gate = pltpu.get_barrier_semaphore()
    for place in range(bits):
        pl.semaphore_signal(gate, inc=1, device_id=(flip(me, 1 << place), core), device_id_type=MESH)
    pl.semaphore_signal(gate, inc=1, device_id=(me, 1 - core), device_id_type=MESH)
    pl.semaphore_wait(gate, bits + 1)


def wait_bytes(region, semaphore):
    pltpu.make_async_copy(region, region, semaphore).wait()


def waves(lanes, last):
    count = max(i + len(lane) for i, lane in enumerate(lanes))
    merged = [
        [lane[at - i] for i, lane in enumerate(lanes) if 0 <= at - i < len(lane)] for at in range(count)
    ]
    return merged + [last]


def run(wave):
    for phase in wave:
        phase()


class Gather:
    def __init__(self, bits, plan, shards, fulls, hop_sems, core_sems, send_sems, own_sems):
        self.bits, self.plan, self.shards, self.fulls = bits, plan, shards, fulls
        self.hop_sems, self.core_sems = hop_sems, core_sems
        self.send_sems, self.own_sems = send_sems, own_sems
        self.me, self.core = lax.axis_index("dp"), lax.axis_index("seq")

    def slot(self, mask):
        return flip_mask(self.me, mask) * 2 + self.core

    def own(self, at, chunk):
        array, first, columns, _ = chunk
        span = pl.ds(first, columns)
        return pltpu.make_async_copy(
            self.shards[array].at[:, span], self.fulls[array].at[self.slot(0), :, span], self.own_sems.at[at]
        )

    def send(self, at, chunk, mask, device, semaphore):
        array, first, columns, _ = chunk
        target = self.fulls[array].at[self.slot(mask), :, pl.ds(first, columns)]
        source = target if mask else self.shards[array].at[:, pl.ds(first, columns)]
        pltpu.make_async_remote_copy(
            src_ref=source, dst_ref=target, send_sem=self.send_sems.at[at],
            recv_sem=semaphore, device_id=device, device_id_type=MESH,
        ).start()

    def region(self, chunk, count):
        array, first, columns, _ = chunk
        return self.fulls[array].at[pl.ds(0, count), :, pl.ds(first, columns)]

    def phase(self, at, chunk, step):
        order = orders_of(self.bits)[chunk[3]]
        masks = masks_of(order)
        fresh = masks[:1] if step == 0 else masks[1 << (step - 1) : 1 << step]
        if step == 0:
            self.own(at, chunk).start()
        else:
            wait_bytes(self.region(chunk, len(fresh)), self.hop_sems.at[at, step - 1])
        if step < self.bits:
            partner = (flip(self.me, 1 << order[step]), self.core)
            for mask in masks[: 1 << step]:
                self.send(at, chunk, mask, partner, self.hop_sems.at[at, step])
        for mask in fresh:
            self.send(at, chunk, mask, (self.me, 1 - self.core), self.core_sems.at[at])

    def finish(self, at, chunk):
        size = 1 << self.bits
        wait_bytes(self.region(chunk, size), self.core_sems.at[at])
        wait_bytes(self.region(chunk, 2 * size - 1), self.send_sems.at[at])
        self.own(at, chunk).wait()

    def waves(self):
        lanes, last, at = [], [], 0
        for lane in self.plan:
            numbered = [(at + i, chunk) for i, chunk in enumerate(lane)]
            at += len(lane)
            lanes.append(
                [partial(self.lane_step, numbered, step) for step in range(self.bits + 1)]
            )
            last += [partial(self.finish, i, chunk) for i, chunk in numbered]
        return waves(lanes, last)

    def lane_step(self, numbered, step):
        for at, chunk in numbered:
            self.phase(at, chunk, step)


def chunks_of(plan):
    return sum(len(lane) for lane in plan)


def gather_scratch(plan, bits):
    count = chunks_of(plan)
    return [
        pltpu.SemaphoreType.DMA((count, bits)),
        pltpu.SemaphoreType.DMA((count,)),
        pltpu.SemaphoreType.DMA((count,)),
        pltpu.SemaphoreType.DMA((count,)),
    ]


def gather_outs(bits, shards):
    return [jax.ShapeDtypeStruct((2 << bits,) + shard.shape, shard.dtype) for shard in shards]


def gather_kernel(bits, plan, count, tokens_ref, *refs):
    shards, (both_ref, *fulls) = refs[:count], refs[count : 2 * count + 1]
    sems = refs[2 * count + 1 : 2 * count + 5]
    token_sems = refs[2 * count + 5]
    me, core = lax.axis_index("dp"), lax.axis_index("seq")
    barrier(bits, me, core)
    steps = Gather(bits, plan, shards, fulls, *sems).waves()
    run(steps[0])
    mine = pltpu.make_async_copy(tokens_ref, both_ref.at[0], token_sems.at[0])
    other = pltpu.make_async_remote_copy(
        src_ref=tokens_ref, dst_ref=both_ref.at[1], send_sem=token_sems.at[1], recv_sem=token_sems.at[2],
        device_id=(me, 1 - core), device_id_type=MESH,
    )
    mine.start()
    other.start()
    for wave in steps[1:]:
        run(wave)
    mine.wait()
    other.wait()


def gather_first(bits, plan, tokens, shards):
    count = len(shards)
    outs = [jax.ShapeDtypeStruct((2,) + tokens.shape, tokens.dtype)] + gather_outs(bits, shards)
    return pl.pallas_call(
        partial(gather_kernel, bits, plan, count),
        out_shape=outs,
        in_specs=[VMEM] * (count + 1),
        out_specs=[ANY] * (count + 1),
        scratch_shapes=gather_scratch(plan, bits) + [pltpu.SemaphoreType.DMA((3,))],
        compiler_params=pltpu.CompilerParams(collective_id=0, has_side_effects=True),
        name="gather_first",
    )(tokens, *shards)


class Scatter:
    def __init__(self, bits, plan, grads, outs, locals_, boxes, box_sems, load_sems, send_sems):
        self.bits, self.plan, self.grads, self.outs, self.locals, self.boxes = bits, plan, grads, outs, locals_, boxes
        self.box_sems, self.load_sems, self.send_sems = box_sems, load_sems, send_sems
        self.me, self.core = lax.axis_index("dp"), lax.axis_index("seq")

    def start(self, at, chunk):
        array, first, columns, which = chunk
        grad, span = self.grads[array], pl.ds(first, columns)
        half = 1 << (self.bits - 1)
        masks = masks_of(orders_of(self.bits)[which])
        for part in (1, 0):
            for place in range(part * half, part * half + half):
                device = flip_mask(self.me, masks[place])
                pltpu.make_async_remote_copy(
                    src_ref=grad.at[device * 2 + 1 - self.core, :, span], dst_ref=self.boxes[at].at[place],
                    send_sem=self.send_sems.at[at], recv_sem=self.box_sems.at[at, part],
                    device_id=(self.me, 1 - self.core), device_id_type=MESH,
                ).start()
                pltpu.make_async_copy(
                    grad.at[device * 2 + self.core, :, span], self.locals[at].at[place], self.load_sems.at[at, part]
                ).start()

    def add(self, at, base, other_ref, other_base, count):
        box = self.boxes[at]

        def one(place, carry):
            total = box[base + place].astype(jnp.float32) + other_ref[other_base + place].astype(jnp.float32)
            box[base + place] = total.astype(jnp.bfloat16)
            return carry

        lax.fori_loop(0, count, one, 0)

    def base(self, step):
        at = 0
        for later in range(self.bits, step, -1):
            at += 1 << later
        return at

    def send(self, at, chunk, step):
        count = 1 << step
        place = orders_of(self.bits)[chunk[3]][step]
        pltpu.make_async_remote_copy(
            src_ref=self.boxes[at].at[pl.ds(self.base(step + 1) + count, count)],
            dst_ref=self.boxes[at].at[pl.ds(self.base(step), count)],
            send_sem=self.send_sems.at[at], recv_sem=self.box_sems.at[at, 2 + step],
            device_id=(flip(self.me, 1 << place), self.core), device_id_type=MESH,
        ).start()

    def halves(self, at, chunk):
        half = 1 << (self.bits - 1)
        for part in (1, 0):
            wait_bytes(self.locals[at].at[pl.ds(0, half)], self.load_sems.at[at, part])
            wait_bytes(self.boxes[at].at[pl.ds(0, half)], self.box_sems.at[at, part])
            self.add(at, part * half, self.locals[at], part * half, half)
            if part:
                self.send(at, chunk, self.bits - 1)

    def step(self, at, chunk, step):
        count = 1 << step
        base, kept = self.base(step), self.base(step + 1)
        wait_bytes(self.boxes[at].at[pl.ds(base, count)], self.box_sems.at[at, 2 + step])
        if step:
            half = count // 2
            self.add(at, base + half, self.boxes[at], kept + half, half)
            self.send(at, chunk, step - 1)
            self.add(at, base, self.boxes[at], kept, half)
        else:
            array, first, columns, _ = chunk
            self.outs[array][:, first : first + columns] = (
                self.boxes[at][base].astype(jnp.float32) + self.boxes[at][kept].astype(jnp.float32)
            )

    def finish(self, at):
        wait_bytes(self.boxes[at].at[pl.ds(0, (2 << self.bits) - 1)], self.send_sems.at[at])

    def lane_step(self, numbered, step):
        for at, chunk in numbered:
            if step == 0:
                self.start(at, chunk)
            elif step == 1:
                self.halves(at, chunk)
            else:
                self.step(at, chunk, self.bits + 1 - step)

    def waves(self):
        lanes, last, at = [], [], 0
        for lane in self.plan:
            numbered = [(at + i, chunk) for i, chunk in enumerate(lane)]
            at += len(lane)
            lanes.append([partial(self.lane_step, numbered, step) for step in range(self.bits + 2)])
            last += [partial(self.finish, i) for i, _ in numbered]
        return waves(lanes, last)


def scatter_scratch(plan, grads, bits):
    size = 1 << bits
    shapes = [(grads[chunk[0]].shape[1], chunk[2]) for lane in plan for chunk in lane]
    count = len(shapes)
    return (
        [pltpu.VMEM((size,) + shape, jnp.bfloat16) for shape in shapes]
        + [pltpu.VMEM((2 * size - 1,) + shape, jnp.bfloat16) for shape in shapes]
        + [
            pltpu.SemaphoreType.DMA((count, bits + 2)),
            pltpu.SemaphoreType.DMA((count, 2)),
            pltpu.SemaphoreType.DMA((count,)),
        ]
    )


def scatter_of(bits, plan, grads, outs, scratch):
    count = chunks_of(plan)
    return Scatter(bits, plan, grads, outs, scratch[:count], scratch[count : 2 * count], *scratch[2 * count :])


def scatter_outs(grads):
    return [jax.ShapeDtypeStruct(grad.shape[1:], jnp.float32) for grad in grads]


def scatter_kernel(bits, plan, count, partial_ref, *refs):
    grads, (other_ref, *outs) = refs[:count], refs[count : 2 * count + 1]
    scratch, swap_sems = refs[2 * count + 1 : -1], refs[-1]
    me, core = lax.axis_index("dp"), lax.axis_index("seq")
    barrier(bits, me, core)
    steps = scatter_of(bits, plan, grads, outs, scratch).waves()
    run(steps[0])
    swap = pltpu.make_async_remote_copy(
        src_ref=partial_ref, dst_ref=other_ref, send_sem=swap_sems.at[0], recv_sem=swap_sems.at[1],
        device_id=(me, 1 - core), device_id_type=MESH,
    )
    swap.start()
    for wave in steps[1:]:
        run(wave)
    swap.wait()


def scatter_last(bits, plan, swapped, grads):
    count = len(grads)
    return pl.pallas_call(
        partial(scatter_kernel, bits, plan, count),
        out_shape=[jax.ShapeDtypeStruct(swapped.shape, swapped.dtype)] + scatter_outs(grads),
        in_specs=[ANY] * (count + 1),
        out_specs=[ANY] + [VMEM] * count,
        scratch_shapes=scatter_scratch(plan, grads, bits) + [pltpu.SemaphoreType.DMA((2,))],
        compiler_params=pltpu.CompilerParams(
            collective_id=1, has_side_effects=True, vmem_limit_bytes=40 * 2**20
        ),
        name="scatter_last",
    )(swapped, *grads)


def whole(shape):
    return pl.BlockSpec(shape, lambda r, p: (0,) * len(shape))


def spread(steps, at, count):
    total = len(steps)
    for i, wave in enumerate(steps):
        pl.when(at == (i * (count - 1)) // (total - 1))(partial(run, wave))


def lane_mask(rows, head):
    lanes = lax.broadcasted_iota(jnp.int32, (rows, PAIR), 1)
    return (lanes // HD) == head


def only(matrix, head):
    return jnp.where(lane_mask(matrix.shape[0], head), matrix, jnp.zeros_like(matrix))


def join_halves(pair_ref, whole_ref, core):
    half = pair_ref.shape[2]
    whole_ref[pl.ds(pl.multiple_of(core * half, half), half)] = pair_ref[0, 0]
    whole_ref[pl.ds(pl.multiple_of((1 - core) * half, half), half)] = pair_ref[1, 0]


def attend_kernel(bits, plan, count, grid, q_ref, k_ref, v_ref, prior_ref, own_ref, all_ref, *refs):
    shards, (logits_ref, context_ref, probs_ref) = refs[:count], refs[count : count + 3]
    fulls, (key_ref, value_ref, score_ref) = refs[count + 3 : 2 * count + 3], refs[2 * count + 3 : 2 * count + 6]
    me, core = lax.axis_index("dp"), lax.axis_index("seq")
    at = pl.program_id(0) * grid[1] + pl.program_id(1)
    pl.when(at == 0)(partial(barrier, bits, me, core))
    spread(Gather(bits, plan, shards, fulls, *refs[2 * count + 6 :]).waves(), at, grid[0] * grid[1])
    join_halves(k_ref, key_ref, core)
    join_halves(v_ref, value_ref, core)
    rows = q_ref.shape[1]
    chunk = 64
    query = q_ref[0] * jnp.bfloat16(HD ** (-0.5))
    for head in range(2):
        score_ref[head] = cols_product(only(query, head), key_ref[...])
    for start in range(0, rows, chunk):
        same = own_ref[0, pl.ds(start, chunk)] == all_ref[0]
        for head in range(2):
            logits = prior_ref[0, head, pl.ds(start, chunk)].astype(jnp.float32) + score_ref[head, pl.ds(start, chunk)]
            logits_ref[0, head, pl.ds(start, chunk)] = logits.astype(jnp.bfloat16)
            masked = jnp.where(same, logits, mask_fill)
            exponent = jnp.exp(masked - jnp.max(masked, -1, keepdims=True))
            weight = 1.0 / jnp.sum(exponent, -1, keepdims=True)
            probs_ref[0, head, pl.ds(start, chunk)] = (exponent * weight).astype(jnp.bfloat16)
    value = value_ref[...]
    context = matmul(probs_ref[0, 0], only(value, 0)) + matmul(probs_ref[0, 1], only(value, 1))
    context_ref[0] = context.astype(jnp.bfloat16)


def attend(bits, plan, queries, keys, values, prev_logits, own_segment, segment_ids, shards):
    rows, qlength, width = queries.shape
    klength = segment_ids.shape[1]
    rect = pl.BlockSpec((1, 2, qlength, klength), lambda r, p: (r, p, 0, 0))
    slim = pl.BlockSpec((1, qlength, PAIR), lambda r, p: (r, 0, p))
    pair = pl.BlockSpec((2, 1, qlength, PAIR), lambda r, p: (0, r, 0, p))
    grid = (rows, width // PAIR)
    return pl.pallas_call(
        partial(attend_kernel, bits, plan, len(shards), grid),
        grid=grid,
        out_shape=[
            jax.ShapeDtypeStruct(prev_logits.shape, jnp.bfloat16),
            jax.ShapeDtypeStruct(queries.shape, jnp.bfloat16),
            jax.ShapeDtypeStruct(prev_logits.shape, jnp.bfloat16),
        ] + gather_outs(bits, shards),
        in_specs=[
            slim, pair, pair, rect,
            pl.BlockSpec((1, qlength, 1), lambda r, p: (r, 0, 0)),
            pl.BlockSpec((1, 1, klength), lambda r, p: (r, 0, 0)),
        ] + [whole(shard.shape) for shard in shards],
        out_specs=[rect, slim, rect] + [ANY] * len(shards),
        scratch_shapes=[
            pltpu.VMEM((klength, PAIR), jnp.bfloat16),
            pltpu.VMEM((klength, PAIR), jnp.bfloat16),
            pltpu.VMEM((2, qlength, klength), jnp.float32),
        ] + gather_scratch(plan, bits),
        compiler_params=pltpu.CompilerParams(
            collective_id=2, has_side_effects=True, vmem_limit_bytes=32 * 2**20
        ),
        name="attend",
    )(queries, keys, values, prev_logits, own_segment[:, :, None], segment_ids[:, None, :], *shards)


def attend_back_kernel(
    bits, plan, count, grid, q_ref, k_ref, v_ref, probs_ref, upstream_ref, context_ref, cotangent_ref, *refs
):
    grads, (logit_grad_ref, query_grad_ref, key_grad_ref, value_grad_ref) = refs[:count], refs[count : count + 4]
    outs, (key_ref, value_ref, score_ref, turn_ref) = refs[count + 4 : 2 * count + 4], refs[2 * count + 4 : 2 * count + 8]
    me, core = lax.axis_index("dp"), lax.axis_index("seq")
    at = pl.program_id(0) * grid[1] + pl.program_id(1)
    pl.when(at == 0)(partial(barrier, bits, me, core))
    spread(scatter_of(bits, plan, grads, outs, refs[2 * count + 8 :]).waves(), at, grid[0] * grid[1])
    join_halves(k_ref, key_ref, core)
    join_halves(v_ref, value_ref, core)
    rows = q_ref.shape[1]
    chunk = 64
    factor = HD ** (-0.5)
    upstream = upstream_ref[0]
    products = upstream.astype(jnp.float32) * context_ref[0].astype(jnp.float32)
    for head in range(2):
        score_ref[head] = cols_product(only(upstream, head), value_ref[...])
    for head in range(2):
        row_dot = jnp.sum(only(products, head), -1, keepdims=True)
        for start in range(0, rows, chunk):
            span = pl.ds(start, chunk)
            probs = probs_ref[0, head, span].astype(jnp.float32)
            grad = cotangent_ref[0, head, span].astype(jnp.float32) + probs * (
                score_ref[head, span] - row_dot[start : start + chunk]
            )
            logit_grad_ref[0, head, span] = grad.astype(jnp.bfloat16)
    key = key_ref[...]
    query_grad = matmul(logit_grad_ref[0, 0], only(key, 0)) + matmul(logit_grad_ref[0, 1], only(key, 1))
    query_grad_ref[0] = (query_grad * factor).astype(jnp.bfloat16)
    query_turned = (q_ref[0].astype(jnp.float32) * factor).T.astype(jnp.bfloat16)
    upstream_turned = upstream.astype(jnp.float32).T.astype(jnp.bfloat16)
    half = key_grad_ref.shape[2]
    for left, right_ref, out_ref in (
        (query_turned, logit_grad_ref, key_grad_ref),
        (upstream_turned, probs_ref, value_grad_ref),
    ):
        for head in range(2):
            turn_ref[head * HD : (head + 1) * HD] = matmul(left[head * HD : (head + 1) * HD], right_ref[0, head])
        score_ref[0, :, :PAIR] = turn_ref[:, :half].T
        score_ref[1, :, :PAIR] = turn_ref[:, half:].T
        out_ref[0, 0] = score_ref[core, :, :PAIR].astype(jnp.bfloat16)
        out_ref[1, 0] = score_ref[1 - core, :, :PAIR].astype(jnp.bfloat16)


def attend_back(bits, plan, queries, keys, values, probs, upstream, context, cotangent, grads):
    rows, qlength, width = queries.shape
    klength = probs.shape[-1]
    rect = pl.BlockSpec((1, 2, qlength, klength), lambda r, p: (r, p, 0, 0))
    slim = pl.BlockSpec((1, qlength, PAIR), lambda r, p: (r, 0, p))
    pair = pl.BlockSpec((2, 1, qlength, PAIR), lambda r, p: (0, r, 0, p))
    grid = (rows, width // PAIR)
    return pl.pallas_call(
        partial(attend_back_kernel, bits, plan, len(grads), grid),
        grid=grid,
        out_shape=[
            jax.ShapeDtypeStruct(cotangent.shape, jnp.bfloat16),
            jax.ShapeDtypeStruct(queries.shape, jnp.bfloat16),
            jax.ShapeDtypeStruct(keys.shape, jnp.bfloat16),
            jax.ShapeDtypeStruct(values.shape, jnp.bfloat16),
        ] + scatter_outs(grads),
        in_specs=[slim, pair, pair, rect, slim, slim, rect] + [ANY] * len(grads),
        out_specs=[rect, slim, pair, pair] + [whole(grad.shape[1:]) for grad in grads],
        scratch_shapes=[
            pltpu.VMEM((klength, PAIR), jnp.bfloat16),
            pltpu.VMEM((klength, PAIR), jnp.bfloat16),
            pltpu.VMEM((2, qlength, klength), jnp.float32),
            pltpu.VMEM((PAIR, klength), jnp.float32),
        ] + scatter_scratch(plan, grads, bits),
        compiler_params=pltpu.CompilerParams(
            collective_id=3, has_side_effects=True, vmem_limit_bytes=50 * 2**20
        ),
        name="attend_back",
    )(queries, keys, values, probs, upstream, context, cotangent, *grads)


LANES = 128


def pack_vectors(rows, wide):
    block = jnp.pad(jnp.stack(rows, -2), ((0, 0),) * (rows[0].ndim - 1) + ((0, 0), (0, LANES - rows[0].shape[-1])))
    long_row = jnp.pad(wide, ((0, 0),) * (wide.ndim - 1) + ((0, LANES - wide.shape[-1]),))[..., None, :]
    block = jnp.concatenate([block, long_row], -2)
    return jnp.pad(block, ((0, 0),) * (block.ndim - 2) + ((0, 16 - block.shape[-2]), (0, 0)))


def body(tokens, prev_logits, segment_ids, out_cotangent, logit_cotangent, *shards):
    seqrows, qlength, width = tokens.shape
    slots = seqrows * qlength
    chips = lax.axis_size("dp")
    bits = chips.bit_length() - 1
    devices = 2 * chips
    (
        querymap, querybias, keymap, valuemap, valuebias, mixmap, mixbias, normgain, normbias,
        expandmap, expandbias, shrinkmap, shrinkbias, outgain, outbias,
    ) = shards
    own = querymap.shape[0]
    hidden = expandmap.shape[1]
    wide = expandbias.shape[0]
    own_segment = lax.dynamic_slice_in_dim(segment_ids, lax.axis_index("seq") * qlength, qlength, 1)

    block = pack_vectors(
        [querybias, valuebias, mixbias, normgain, normbias, shrinkbias, outgain, outbias], expandbias
    )
    thin, third, part = (width // 2) // LANES * LANES, hidden // 3, width // 3
    both_tokens, querymap, keymap, valuemap, block = gather_first(
        bits,
        [
            [(0, 0, width, 0), (1, 0, width, 1)],
            [(2, 0, thin, 0), (2, thin, width - thin, 1), (3, 0, LANES, 0)],
        ],
        tokens,
        [querymap, keymap, valuemap, block],
    )
    querymap, keymap, valuemap = [m.reshape(width, width) for m in (querymap, keymap, valuemap)]
    rows = block[:, :8, :own].transpose(1, 0, 2).reshape(8, width)
    rows, expandbias = lax.optimization_barrier((rows, block[:, 8, :wide].reshape(1, hidden)))
    querybias, valuebias, mixbias, normgain, normbias, shrinkbias, outgain, outbias = [
        rows[i : i + 1].astype(jnp.float32) for i in range(8)
    ]
    expandbias = expandbias.astype(jnp.float32)

    token_rows = tokens.reshape(slots, width)
    both_rows = both_tokens.reshape(2 * slots, width)
    queries = (matmul(token_rows, querymap) + querybias).astype(jnp.bfloat16).reshape(seqrows, qlength, width)
    keys = matmul(both_rows, keymap).astype(jnp.bfloat16).reshape(2, seqrows, qlength, width)
    values = (matmul(both_rows, valuemap) + valuebias).astype(jnp.bfloat16).reshape(2, seqrows, qlength, width)
    raw_logits, context_heads, probs, mixmap, expandmap, shrinkmap = attend(
        bits,
        [[(0, 0, width, 0)]]
        + [[(1, i * third, third, 0), (2, i * part, part, 1)] for i in range(3)],
        queries, keys, values, prev_logits, own_segment, segment_ids, [mixmap, expandmap, shrinkmap],
    )
    mixmap = mixmap.reshape(width, width)
    expandmap = expandmap.reshape(width, hidden)
    shrinkmap = shrinkmap.reshape(hidden, width)
    context = context_heads.reshape(slots, width)
    attended = matmul(context, mixmap) + mixbias
    unit_first, scale_first = normalize(token_rows.astype(jnp.float32) + attended)
    normed = (unit_first * normgain + normbias).astype(jnp.bfloat16)
    inner_pre = matmul(normed, expandmap) + expandbias
    active, gelu_slope = jax.jvp(
        partial(jax.nn.gelu, approximate=False), (inner_pre,), (jnp.ones_like(inner_pre),)
    )
    active = active.astype(jnp.bfloat16)
    gelu_slope = gelu_slope.astype(jnp.bfloat16)
    second = normed.astype(jnp.float32) + (matmul(active, shrinkmap) + shrinkbias)
    unit_second, scale_second = normalize(second)
    layer_out = unit_second * outgain + outbias

    upstream = out_cotangent.reshape(slots, width).astype(jnp.float32)
    outgain_grad = jnp.sum(upstream * unit_second, 0)
    outbias_grad = jnp.sum(upstream, 0)
    second_grad = norm_back(upstream, unit_second, scale_second, outgain)
    branch_grad = second_grad.astype(jnp.bfloat16)
    shrinkbias_grad = column_sum(branch_grad)
    shrinkmap_grad = rows_product(active, branch_grad).astype(jnp.bfloat16)
    active_grad = cols_product(branch_grad, shrinkmap)
    inner_grad = (active_grad * gelu_slope.astype(jnp.float32)).astype(jnp.bfloat16)
    expandbias_grad = column_sum(inner_grad)
    expandmap_grad = rows_product(normed, inner_grad).astype(jnp.bfloat16)
    normed_grad = second_grad + cols_product(inner_grad, expandmap)
    normgain_grad = jnp.sum(normed_grad * unit_first, 0)
    normbias_grad = jnp.sum(normed_grad, 0)
    first_grad = norm_back(normed_grad, unit_first, scale_first, normgain)
    attended_grad = first_grad.astype(jnp.bfloat16)
    mixbias_grad = column_sum(attended_grad)
    mixmap_grad = rows_product(context, attended_grad).astype(jnp.bfloat16)
    context_grad = cols_product(attended_grad, mixmap).astype(jnp.bfloat16).reshape(seqrows, qlength, width)
    logits_grad, query_grad, key_grad, value_grad, mixmap_grad, expandmap_grad, shrinkmap_grad = attend_back(
        bits,
        [[(1, i * third, third, 0), (2, i * part, part, 1)] for i in range(3)] + [[(0, 0, width, 0)]],
        queries, keys, values, probs, context_grad, context_heads, logit_cotangent,
        [
            mixmap_grad.reshape(devices, own, width),
            expandmap_grad.reshape(devices, own, hidden),
            shrinkmap_grad.reshape(devices, wide, width),
        ],
    )
    query_grad = query_grad.reshape(slots, width)
    key_grad = key_grad.reshape(2 * slots, width)
    value_grad = value_grad.reshape(2 * slots, width)
    other_grad = (
        cols_product(key_grad[slots:], keymap) + cols_product(value_grad[slots:], valuemap)
    ).astype(jnp.bfloat16)
    querymap_grad = rows_product(token_rows, query_grad).astype(jnp.bfloat16)
    querybias_grad = column_sum(query_grad)
    keymap_grad = rows_product(both_rows, key_grad).astype(jnp.bfloat16)
    valuemap_grad = rows_product(both_rows, value_grad).astype(jnp.bfloat16)
    valuebias_grad = column_sum(value_grad)
    tokens_grad = (
        first_grad
        + cols_product(query_grad, querymap)
        + cols_product(key_grad[:slots], keymap)
        + cols_product(value_grad[:slots], valuemap)
    )
    stacked = lax.optimization_barrier(
        jnp.stack(
            [
                querybias_grad, valuebias_grad, mixbias_grad, normgain_grad, normbias_grad,
                shrinkbias_grad, outgain_grad, outbias_grad,
            ]
        )
    ).reshape(8, devices, own).transpose(1, 0, 2)
    block = pack_vectors([stacked[:, i] for i in range(8)], expandbias_grad.reshape(devices, wide)).astype(jnp.bfloat16)
    swapped, querymap_grad, keymap_grad, valuemap_grad, block = scatter_last(
        bits,
        [
            [(0, 0, width, 0), (1, 0, width, 1)],
            [(2, 0, thin, 0), (2, thin, width - thin, 1), (3, 0, LANES, 0)],
        ],
        other_grad,
        [
            querymap_grad.reshape(devices, own, width),
            keymap_grad.reshape(devices, own, width),
            valuemap_grad.reshape(devices, own, width),
            block,
        ],
    )
    tokens_grad = tokens_grad + swapped.astype(jnp.float32)
    (
        querybias_grad, valuebias_grad, mixbias_grad, normgain_grad, normbias_grad,
        shrinkbias_grad, outgain_grad, outbias_grad,
    ) = [block[i, :own] for i in range(8)]
    expandbias_grad = block[8, :wide]
    return (
        layer_out.reshape(seqrows, qlength, width).astype(jnp.bfloat16),
        raw_logits,
        tokens_grad.reshape(seqrows, qlength, width).astype(jnp.bfloat16),
        logits_grad,
        querymap_grad, querybias_grad, keymap_grad, valuemap_grad, valuebias_grad,
        mixmap_grad, mixbias_grad, normgain_grad, normbias_grad,
        expandmap_grad, expandbias_grad, shrinkmap_grad, shrinkbias_grad,
        outgain_grad, outbias_grad,
    )


def solution(mesh):
    in_specs = (
        P("dp", "seq", None),
        P("dp", None, "seq", None),
        P("dp", None),
        P("dp", "seq", None),
        P("dp", None, "seq", None),
        P(("dp", "seq"), None),
        P(("dp", "seq")),
        P(("dp", "seq"), None),
        P(("dp", "seq"), None),
        P(("dp", "seq")),
        P(("dp", "seq"), None),
        P(("dp", "seq")),
        P(("dp", "seq")),
        P(("dp", "seq")),
        P(("dp", "seq"), None),
        P(("dp", "seq")),
        P(("dp", "seq"), None),
        P(("dp", "seq")),
        P(("dp", "seq")),
        P(("dp", "seq")),
    )
    out_specs = (
        P("dp", "seq", None),
        P("dp", None, "seq", None),
        P("dp", "seq", None),
        P("dp", None, "seq", None),
        P(("dp", "seq"), None),
        P(("dp", "seq")),
        P(("dp", "seq"), None),
        P(("dp", "seq"), None),
        P(("dp", "seq")),
        P(("dp", "seq"), None),
        P(("dp", "seq")),
        P(("dp", "seq")),
        P(("dp", "seq")),
        P(("dp", "seq"), None),
        P(("dp", "seq")),
        P(("dp", "seq"), None),
        P(("dp", "seq")),
        P(("dp", "seq")),
        P(("dp", "seq")),
    )
    return jax.shard_map(body, mesh=mesh, in_specs=in_specs, out_specs=out_specs, check_vma=False)
```
